512 devices in a mesh: fx: 16 (over z), fy: 8 (over y, core), ma: 4 (over x).
Axes of the slice: x: 4, y: 4, z: 16, core: 2. Of those that a mesh axis runs over, the one named last changes fastest.
Arguments:
- efield_vector: float32 [3, 32, 512, 1024], P(None, 'ma', 'fx', 'fy'), may hold values from -6 to 6
- hfield_vector: float32 [3, 32, 512, 1024], P(None, 'ma', 'fx', 'fy'), may hold values from -6 to 6
- statistical_operator: float32 [16, 768, 64, 128], P('fx', ('fy', 'ma')), may hold values from -6 to 6
- population_grid: float32 [16, 768, 128], P('fx', ('fy', 'ma')), may hold values from 0.5 to 1.5
- patch_placement: int32 [16, 768], P('fx', ('fy', 'ma')), may hold values from 0 to 63, as said below
- departure_lines: int32 [16, 32, 32, 2], P('fx', ('fy', 'ma')), may hold values from 0 to 255, as said below
- generator_stack: float32 [5, 64, 64], replicated, may hold values from -0.36 to 0.36
- moment_vector: float32 [3, 64], replicated, may hold values from -0.75 to 0.75
- drain_shares: float32 [64], replicated, may hold values from -0.75 to 0.75
Outputs:
- electric_out: float32 [3, 32, 512, 1024], P(None, 'ma', 'fx', 'fy')
- magnetic_out: float32 [3, 32, 512, 1024], P(None, 'ma', 'fx', 'fy')
- density_out: float32 [16, 768, 64, 128], P('fx', ('fy', 'ma'))
- carriers_out: float32 [16, 768, 128], P('fx', ('fy', 'ma'))
The draws below stay inside these ranges and needn't reach their ends.
Inputs may be any that keep to these rules, and one draw needn't show every extreme that they name: `patch_placement`: for each index c of fx and owner m, the 24 entries are distinct slots s * 2 + k: the owner takes k = 0 .. 1 from each of 12 different sources s and nothing from other sources. In each index of fx some sources are taken by every owner. departure_lines[c, s, m, k] is a local row z * 32 + x of source block s at index c of fx. Where owner m takes slot s * 2 + k it is that tile's row, and these rows are distinct over all such (m, k) of one source; other entries name some row and carry no tile.
All inputs are finite; a program needn't handle non-finite values.
Results may differ from the reference program's by a relative error of at most 0.00014.
Values sent between devices are 32-bit elements; how exact they have to be, the bound alone decides.
A program may use at most 64 MiB of HBM per device.

```python
import jax
import jax.numpy as jnp
from jax import lax

CZ = 8
CX = 32
PATCH_HEIGHT = 128
PATCHES_HELD = 24
STEPS = 2
LIOU = 64
SENDER_COUNT = 32
CAP = 2
NZ = 32
NX = 512
NY = 1024
N_FX = 16
N_FY = 8
N_MA = 4


def routing_tables(key):
    base_key = jax.random.fold_in(key, 1234)
    key_hot, key_score, key_rows = jax.random.split(base_key, 3)
    groups = PATCHES_HELD // CAP
    hot_count = max(1, groups // 4)
    rows_total = CZ * CX
    source_iota = jnp.arange(SENDER_COUNT, dtype=jnp.int32)
    hot_score = jax.random.randint(key_hot, (N_FX, SENDER_COUNT), 0, 1 << 20, dtype=jnp.int32) * SENDER_COUNT + source_iota[None, :]
    hot_values, hot_picks = lax.top_k(hot_score, hot_count)
    hot_flag = jnp.sum((hot_picks[:, :, None] == source_iota[None, None, :]).astype(jnp.int32), axis=1)
    scores = (jax.random.randint(key_score, (N_FX, SENDER_COUNT, SENDER_COUNT), 0, 1 << 12, dtype=jnp.int32) + hot_flag[:, None, :] * (1 << 13)) * SENDER_COUNT + source_iota[None, None, :]
    score_values, chosen = lax.top_k(scores, groups)
    chosen = chosen.astype(jnp.int32)
    requested = jnp.sum((chosen[:, :, :, None] == source_iota[None, None, None, :]).astype(jnp.int32), axis=2)
    offset = jnp.cumsum(requested, axis=1) - requested
    row_score = jax.random.randint(key_rows, (N_FX, SENDER_COUNT, rows_total), 0, 1 << 16, dtype=jnp.int32) * rows_total + jnp.arange(rows_total, dtype=jnp.int32)[None, None, :]
    row_perm = jnp.argsort(row_score, axis=2).astype(jnp.int32)
    position = jnp.transpose(offset, (0, 2, 1))[:, :, :, None] * CAP + jnp.arange(CAP, dtype=jnp.int32)[None, None, None, :]
    departure_lines = jnp.take_along_axis(row_perm, position.reshape(N_FX, SENDER_COUNT, SENDER_COUNT * CAP), axis=2).reshape(N_FX, SENDER_COUNT, SENDER_COUNT, CAP)
    patch_placement = (chosen[:, :, :, None] * CAP + jnp.arange(CAP, dtype=jnp.int32)[None, None, None, :]).reshape(N_FX, SENDER_COUNT * PATCHES_HELD)
    return (patch_placement.astype(jnp.int32), departure_lines.astype(jnp.int32))


def draw_patch_placement(key, part):
    return routing_tables(key)[0]


def draw_departure_lines(key, part):
    return routing_tables(key)[1]


def level_of(stream_key, dims, cuts, least, top_value):
    gain = 1.0
    for dim, blocks in cuts:
        draws = jax.random.uniform(jax.random.fold_in(jax.random.fold_in(stream_key, 6), dim), (blocks,), jnp.float32, least / len(cuts), top_value / len(cuts))
        gain = gain * jnp.repeat(jnp.exp(draws), dims[dim] // blocks).reshape((-1,) + (1,) * (len(dims) - 1 - dim))
    return gain


def noise(stream_key, dims, scale, limit, pieces=(), kind=jnp.bfloat16):
    level = level_of(stream_key, dims, pieces, -0.22, 0.18) if pieces else 1.0
    result = jax.random.normal(stream_key, dims, jnp.float32) * scale * level
    return jnp.minimum(jnp.maximum(result, -limit), limit).astype(kind)


def setup_inputs(seed: int = 0) -> dict:
    seeds = jax.random.split(jax.random.key(seed), 10)
    return {
        "efield_vector": noise(seeds[0], (3, NZ, NX, NY), 1.0, 6.0, ((1, 4), (2, 16), (3, 8)), jnp.float32),
        "hfield_vector": noise(seeds[1], (3, NZ, NX, NY), 1.0, 6.0, ((1, 4), (2, 16), (3, 8)), jnp.float32),
        "statistical_operator": noise(seeds[2], (N_FX, SENDER_COUNT * PATCHES_HELD, LIOU, PATCH_HEIGHT), 1.0, 6.0, ((0, 16), (1, 32)), jnp.float32),
        "population_grid": jnp.clip(0.5 + 1.0 * jax.random.uniform(seeds[3], (N_FX, SENDER_COUNT * PATCHES_HELD, PATCH_HEIGHT), jnp.float32) ** level_of(seeds[3], (N_FX, SENDER_COUNT * PATCHES_HELD, PATCH_HEIGHT), ((0, 16), (1, 32)), -0.2, 0.2), 0.5, 1.5),
        "patch_placement": draw_patch_placement(jax.random.fold_in(seeds[9], 71), 0),
        "departure_lines": draw_departure_lines(jax.random.fold_in(seeds[9], 71), 0),
        "generator_stack": noise(seeds[6], (5, LIOU, LIOU), 0.06, 0.36, (), jnp.float32),
        "moment_vector": noise(seeds[7], (3, LIOU), LIOU ** -0.5, 0.75, (), jnp.float32),
        "drain_shares": noise(seeds[8], (LIOU,), LIOU ** -0.5, 0.75, (), jnp.float32),
    }


interval_length = 0.5
population_diffusion = 0.25
attenuation_factors = 0.1
relaxation_speed = 0.5


def assemble(diff_z, diff_x, diff_y):
    curl_x = diff_y[2] - diff_z[1]
    curl_y = diff_z[0] - diff_x[2]
    curl_z = diff_x[1] - diff_y[0]
    return jnp.stack([curl_x, curl_y, curl_z], axis=0)


def forward_curl(field_grid, extent):
    cells_z, cells_x, cells_y = extent
    center = field_grid[:, :cells_z, :cells_x, :cells_y]
    diff_z = field_grid[:, 1:cells_z + 1, :cells_x, :cells_y] - center
    diff_x = field_grid[:, :cells_z, 1:cells_x + 1, :cells_y] - center
    diff_y = field_grid[:, :cells_z, :cells_x, 1:cells_y + 1] - center
    return assemble(diff_z, diff_x, diff_y)


def backward_curl(field_grid, extent):
    cells_z, cells_x, cells_y = extent
    center = field_grid[:, 1:cells_z + 1, 1:cells_x + 1, 1:cells_y + 1]
    diff_z = center - field_grid[:, :cells_z, 1:cells_x + 1, 1:cells_y + 1]
    diff_x = center - field_grid[:, 1:cells_z + 1, :cells_x, 1:cells_y + 1]
    diff_y = center - field_grid[:, 1:cells_z + 1, 1:cells_x + 1, :cells_y]
    return assemble(diff_z, diff_x, diff_y)


def rate_terms(dipole_flux, difference_coefficients, generator_stack):
    products = jnp.einsum("aml,tly->atmy", generator_stack, dipole_flux, precision=lax.Precision.HIGHEST)
    return jnp.einsum("aty,atmy->tmy", difference_coefficients, products, precision=lax.Precision.HIGHEST)


def medium_update(dipole_flux, population_now, partitioned_grids, generator_stack, moment_vector, drain_shares):
    difference_coefficients = jnp.concatenate([jnp.ones_like(population_now)[None], population_now[None], partitioned_grids], axis=0)
    slope_one = rate_terms(dipole_flux, difference_coefficients, generator_stack)
    slope_two = rate_terms(dipole_flux + (0.5 * interval_length) * slope_one, difference_coefficients, generator_stack)
    slope_three = rate_terms(dipole_flux + (0.5 * interval_length) * slope_two, difference_coefficients, generator_stack)
    slope_four = rate_terms(dipole_flux + interval_length * slope_three, difference_coefficients, generator_stack)
    evolved_state = dipole_flux + (interval_length / 6.0) * (slope_one + 2.0 * slope_two + 2.0 * slope_three + slope_four)
    injection_strength = jnp.einsum("l,tly->ty", drain_shares, dipole_flux, precision=lax.Precision.HIGHEST)
    bordered_patches = jnp.pad(population_now, ((0, 0), (1, 1)), mode="edge")
    curvature_term = bordered_patches[:, 2:] - 2.0 * population_now + bordered_patches[:, :-2]
    population_next = population_now + interval_length * (population_diffusion * curvature_term - attenuation_factors * population_now - relaxation_speed * population_now * injection_strength)
    operator_delta = jnp.einsum("pl,tly->pty", moment_vector, evolved_state - dipole_flux, precision=lax.Precision.HIGHEST)
    return evolved_state, population_next, operator_delta


def reference(efield_vector, hfield_vector, statistical_operator, population_grid, patch_placement, departure_lines, generator_stack, moment_vector, drain_shares):
    tile_count = SENDER_COUNT * PATCHES_HELD
    column = jnp.broadcast_to(jnp.arange(N_FX, dtype=jnp.int32)[:, None], (N_FX, tile_count))
    matter = jnp.broadcast_to((jnp.arange(tile_count, dtype=jnp.int32) // PATCHES_HELD)[None, :], (N_FX, tile_count))
    source = patch_placement // CAP
    within = patch_placement % CAP
    row_local = departure_lines[column, source, matter, within]
    plane_index = (source % N_MA) * CZ + row_local // CX
    line_index = column * CX + row_local % CX
    block_index = source // N_MA

    def lattice_update(items):
        return medium_update(items[0], items[1], items[2], generator_stack, moment_vector, drain_shares)

    dipole_flux = statistical_operator
    population_now = population_grid
    efield_now = efield_vector
    hfield_now = hfield_vector
    extent = (NZ, NX, NY)
    for step_index in range(STEPS):
        blocks = efield_now.reshape(3, NZ, NX, N_FY, PATCH_HEIGHT)
        partitioned_grids = jnp.moveaxis(blocks[:, plane_index, line_index, block_index, :], 0, 1)
        dipole_flux, population_now, operator_delta = lax.map(lattice_update, (dipole_flux, population_now, partitioned_grids))
        change_grid = jnp.zeros((3, NZ, NX, N_FY, PATCH_HEIGHT), jnp.float32).at[:, plane_index, line_index, block_index, :].add(jnp.moveaxis(operator_delta, 1, 0)).reshape(3, NZ, NX, NY)
        bordered_patches = jnp.pad(efield_now, ((0, 0), (0, 1), (0, 1), (0, 1)))
        hfield_now = hfield_now - interval_length * forward_curl(bordered_patches, extent)
        bordered_patches = jnp.pad(hfield_now, ((0, 0), (1, 0), (1, 0), (1, 0)))
        efield_now = efield_now + interval_length * backward_curl(bordered_patches, extent) - change_grid
    return efield_now, hfield_now, dipole_flux, population_now
```

```python
import functools

import jax
import jax.numpy as jnp
from jax import lax
from jax.experimental import pallas as pl
from jax.experimental.pallas import tpu as pltpu
from jax.sharding import PartitionSpec as P

MESH = pl.DeviceIdType.MESH
F32 = jnp.float32
BF16 = jnp.bfloat16
H_STEP = 0.5
DIFFUSION = 0.25
ATTENUATION = 0.1
RELAXATION = 0.5
LANES = 128
CZ, CX, LIOU = 8, 32, 64
PLANE = CZ * CX
GROUP = 4


def split(x):
    hi = x.astype(BF16)
    return hi, (x - hi.astype(F32)).astype(BF16)


def stacked(x):
    hi, lo = split(x)
    return jnp.concatenate([hi, lo, hi], axis=0)


def lane_iota(shape):
    return lax.broadcasted_iota(jnp.int32, shape, len(shape) - 1)


def widen(x):
    hi, lo = split(x)
    row = lax.broadcasted_iota(jnp.int32, (LIOU, 3 * LIOU), 0)
    col = lane_iota((LIOU, 3 * LIOU))
    high = jnp.where((col < 2 * LIOU) & (col % LIOU == row), 1.0, 0.0).astype(BF16)
    low = jnp.where(col == row + 2 * LIOU, 1.0, 0.0).astype(BF16)
    out = jnp.dot(hi, high, preferred_element_type=F32) + jnp.dot(
        lo, low, preferred_element_type=F32
    )
    return out.astype(BF16)


def medium(tiles, q, qarg, kacc, coef, gen, mom, inj, dp):
    pairs = tiles // 2
    group = GROUP if pairs % GROUP == 0 else 1

    def run(first):
        def both(ref, p, rows, offset=0, size=None):
            size = rows if size is None else size
            base = (first + p) * 2 * rows + offset
            return jnp.concatenate(
                [ref[pl.ds(base, size), :], ref[pl.ds(base + rows, size), :]], axis=1
            )

        def put(ref, p, rows, value):
            base = (first + p) * 2 * rows
            ref[pl.ds(base, rows), :] = value[:, :LANES]
            ref[pl.ds(base + rows, rows), :] = value[:, LANES:]

        for stage in range(4):
            for p in range(group):
                arg = both(q if stage == 0 else qarg, p, LIOU)
                rows = 5 * LIOU + (16 if stage == 0 else 0)
                prod = jnp.dot(gen[:rows, :], stacked(arg), preferred_element_type=F32)
                c = [both(coef, p, 8, a, 1) for a in range(4)]
                parts = []
                for j in range(LIOU // 8):
                    b = j * 40
                    part = prod[b : b + 8]
                    for a in range(4):
                        part = part + c[a] * prod[b + 8 * a + 8 : b + 8 * a + 16]
                    parts.append(part)
                k = jnp.concatenate(parts, axis=0)
                if stage == 0:
                    put(inj, p, 8, prod[5 * LIOU : 5 * LIOU + 8])
                    put(kacc, p, LIOU, k)
                    put(qarg, p, LIOU, arg + (0.5 * H_STEP) * k)
                elif stage < 3:
                    put(kacc, p, LIOU, both(kacc, p, LIOU) + 2.0 * k)
                    step = 0.5 * H_STEP if stage == 1 else H_STEP
                    put(qarg, p, LIOU, both(q, p, LIOU) + step * k)
                else:
                    old = both(q, p, LIOU)
                    new = old + (H_STEP / 6.0) * (both(kacc, p, LIOU) + k)
                    put(q, p, LIOU, new)
                    change = jnp.dot(mom[...], stacked(new - old), preferred_element_type=F32)
                    put(dp, p, 8, change[:8])

    if group == pairs:
        run(0)
    else:
        lax.fori_loop(0, pairs // group, lambda g, carry: (run(g * group), carry)[1], 0)


def kernel(
    nfx, nfy, nma, tiles,
    rows_s, slots_s, e_in, h_in, q_in, n_in, l_in, m_in, d_in,
    e_out, h_out, q_out, n_out,
    e, h, q, qarg, kacc, pop, coef, inj, dp, gen, mom, lperm, pick, drop, grid,
    xs0, xs1, xs2, xs3, xr0, xr1, xr2, xr3, zs, zr, ls, lr, ys, yr,
    load_sem, save_sem, xs_sem, xr_sem, fs_sem, fr_sem,
):
    senders = nfy * nma
    fx, fy, ma = lax.axis_index("fx"), lax.axis_index("fy"), lax.axis_index("ma")
    me = fy * nma + ma
    xs, xr = (xs0, xs1, xs2, xs3), (xr0, xr1, xr2, xr3)

    loads = [
        pltpu.make_async_copy(src, dst, load_sem.at[i])
        for i, (src, dst) in enumerate(((e_in, e), (h_in, h), (q_in, q), (n_in, pop)))
    ]
    for copy in loads:
        copy.start()

    barrier = pltpu.get_barrier_semaphore()

    def greet(d, carry):
        m = lax.rem(me + d, senders)
        pl.semaphore_signal(
            barrier, inc=1, device_id=(fx, m // nma, lax.rem(m, nma)), device_id_type=MESH
        )
        return carry

    lax.fori_loop(1, senders, greet, 0)
    for d in (1, nfx - 1):
        pl.semaphore_signal(
            barrier, inc=1, device_id=(lax.rem(fx + d, nfx), fy, ma), device_id_type=MESH
        )

    def gather(i):
        xs[i][...] = jnp.zeros((senders * 8, LANES), F32)

        def body(m, carry):
            for k in range(2):
                r = rows_s[0, 0, m, k]
                for c in range(3):
                    xs[i][pl.ds(m * 8 + k * 4 + c, 1), :] = e[pl.ds(c * PLANE + r, 1), :]
            return carry

        lax.fori_loop(0, senders, body, 0)

    def send(i):
        own = pl.ds(pl.multiple_of(me * 8, 8), 8)
        xr[i][own, :] = xs[i][own, :]

        def body(d, carry):
            m = lax.rem(me + d, senders)
            pltpu.make_async_remote_copy(
                src_ref=xs[i].at[pl.ds(pl.multiple_of(m * 8, 8), 8)],
                dst_ref=xr[i].at[own],
                send_sem=xs_sem.at[i],
                recv_sem=xr_sem.at[i],
                device_id=(fx, m // nma, lax.rem(m, nma)),
                device_id_type=MESH,
            ).start()
            return carry

        lax.fori_loop(1, senders, body, 0)

    def arrived(i):
        whole = pl.ds(0, (senders - 1) * 8)
        return pltpu.make_async_remote_copy(
            src_ref=xs[i].at[whole],
            dst_ref=xr[i].at[whole],
            send_sem=xs_sem.at[i],
            recv_sem=xr_sem.at[i],
            device_id=(fx, fy, ma),
            device_id_type=MESH,
        )

    lane8 = lane_iota((8, LANES))

    def faces(i, f, low):
        z = 0 if low else CZ - 1
        x = 0 if low else CX - 1
        y = 0 if low else LANES - 1
        for n, c in enumerate((0, 1)):
            zs[i, n * CX : (n + 1) * CX, :] = f[c * PLANE + z * CX : c * PLANE + (z + 1) * CX, :]
        for n, c in enumerate((1, 2)):
            for p in range(CZ):
                ls[i, n * CZ + p : n * CZ + p + 1, :] = f[pl.ds(c * PLANE + p * CX + x, 1), :]
        pack = jnp.zeros((8, LANES), F32)
        for n, c in enumerate((0, 2)):
            for g in range(CZ * CX // 8):
                piece = f[c * PLANE + g * 8 : c * PLANE + g * 8 + 8, :]
                pack = jnp.where(lane8 == n * 32 + g, piece[:, y : y + 1], pack)
        ys[i] = pack

    def face_copies(i, low):
        def to(index, size):
            return lax.rem(index + (size - 1 if low else 1), size)

        targets = (
            (zs, zr, (fx, fy, to(ma, nma))),
            (ls, lr, (to(fx, nfx), fy, ma)),
            (ys, yr, (fx, to(fy, nfy), ma)),
        )
        return [
            pltpu.make_async_remote_copy(
                src_ref=src.at[i],
                dst_ref=dst.at[i],
                send_sem=fs_sem.at[i, n],
                recv_sem=fr_sem.at[i, n],
                device_id=device,
                device_id_type=MESH,
            )
            for n, (src, dst, device) in enumerate(targets)
        ]

    row32 = lax.broadcasted_iota(jnp.int32, (CX, LANES), 0)
    lane32 = lane_iota((CX, LANES))

    def curl(i, f, forward):
        if forward:
            live = (ma < nma - 1, fx < nfx - 1, fy < nfy - 1)
        else:
            live = (ma > 0, fx > 0, fy > 0)
        live = [jnp.where(flag, 1.0, 0.0).astype(F32) for flag in live]
        shift_x, shift_y = (CX - 1, LANES - 1) if forward else (1, 1)
        edge_x, edge_y = (CX - 1, LANES - 1) if forward else (0, 0)
        packed = yr[i] * live[2]

        def plane(c, z):
            return f[c * PLANE + z * CX : c * PLANE + (z + 1) * CX, :]

        def diff(other, here):
            return other - here if forward else here - other

        for z in range(CZ):
            fields = [plane(c, z) for c in range(3)]

            def dz(c):
                n = z + (1 if forward else -1)
                if 0 <= n < CZ:
                    other = plane(c, n)
                else:
                    other = zr[i, c * CX : (c + 1) * CX, :] * live[0]
                return diff(other, fields[c])

            def dx(c):
                n = (c - 1) * CZ + z
                other = pltpu.roll(fields[c], shift_x, 0)
                other = jnp.where(row32 == edge_x, lr[i, n : n + 1, :] * live[1], other)
                return diff(other, fields[c])

            def dy(c):
                n = (c // 2) * 32 + z * 4
                other = pltpu.roll(fields[c], shift_y, 1)
                column = jnp.concatenate([packed[:, n + g : n + g + 1] for g in range(4)], axis=0)
                other = jnp.where(lane32 == edge_y, column, other)
                return diff(other, fields[c])

            yield 0, z, dy(2) - dz(1)
            yield 1, z, dz(0) - dx(2)
            yield 2, z, dx(1) - dy(0)

    def advance(i, target, source, forward):
        sign = -H_STEP if forward else H_STEP
        for c, z, value in curl(i, source, forward):
            at = slice(c * PLANE + z * CX, c * PLANE + (z + 1) * CX)
            target[at, :] = target[at, :] + sign * value

    def coefficients(i, with_change):
        def body(t, carry):
            s4 = slots_s[0, t] * 4
            coef[pl.ds(t * 8, 1), :] = pop[pl.ds(t, 1), :]
            for c in range(3):
                value = xr[i][pl.ds(s4 + c, 1), :]
                if with_change:
                    value = value - dp[pl.ds(t * 8 + c, 1), :]
                coef[pl.ds(t * 8 + 1 + c, 1), :] = value
            return carry

        lax.fori_loop(0, tiles, body, 0)

    def carriers():
        now = pop[...]
        drain = jnp.concatenate([inj[t * 8 : t * 8 + 1, :] for t in range(tiles)], axis=0)
        lane = lane_iota((tiles, LANES))
        after = jnp.where(lane == LANES - 1, now, pltpu.roll(now, LANES - 1, 1))
        before = jnp.where(lane == 0, now, pltpu.roll(now, 1, 1))
        pop[...] = now + H_STEP * (
            DIFFUSION * (after - 2.0 * now + before)
            - ATTENUATION * now
            - RELAXATION * now * drain
        )

    def give_back(i):
        hi, lo = split(dp[...])
        xs[i][...] = jnp.dot(pick[...], hi, preferred_element_type=F32) + jnp.dot(
            pick[...], lo, preferred_element_type=F32
        )

    def subtract_change(i):
        back = xr[i][...]
        part = lax.broadcasted_iota(jnp.int32, back.shape, 0) % 4
        for c in range(3):
            hi, lo = split(jnp.where(part == c, back, 0.0))
            change = jnp.dot(drop[...], hi, preferred_element_type=F32) + jnp.dot(
                drop[...], lo, preferred_element_type=F32
            )
            at = slice(c * PLANE, (c + 1) * PLANE)
            e[at, :] = e[at, :] - change

    def prepare():
        for a in range(5):
            for j in range(LIOU // 8):
                lperm[j * 40 + a * 8 : j * 40 + a * 8 + 8, :] = l_in[a, j * 8 : j * 8 + 8, :]
        lperm[5 * LIOU :, :] = jnp.zeros((16, LIOU), F32)
        lperm[5 * LIOU : 5 * LIOU + 1, :] = d_in[...]
        gen[...] = widen(lperm[...])
        lperm[:16, :] = jnp.zeros((16, LIOU), F32)
        lperm[:3, :] = m_in[...]
        mom[...] = widen(lperm[:16, :])
        lane = lane_iota((8, tiles * 8))
        where_to = jnp.zeros((8, tiles * 8), jnp.int32)
        for t in range(tiles):
            where_to = jnp.where(lane // 8 == t, slots_s[0, t] * 4, where_to)
        where_to = where_to + lane % 8
        for g in range(senders):
            row = lax.broadcasted_iota(jnp.int32, (8, tiles * 8), 0) + g * 8
            lperm_free = jnp.where(where_to == row, 1.0, 0.0)
            grid[g * 8 : g * 8 + 8, : tiles * 8] = lperm_free
        pick[...] = grid[: senders * 8, : tiles * 8].astype(BF16)
        lane = lane_iota((8, senders * 8))
        line = jnp.zeros((8, senders * 8), jnp.int32)
        for m in range(senders):
            for k in range(2):
                line = jnp.where(lane // 4 == m * 2 + k, rows_s[0, 0, m, k], line)
        for g in range(PLANE // 8):
            row = lax.broadcasted_iota(jnp.int32, (8, senders * 8), 0) + g * 8
            grid[g * 8 : g * 8 + 8, : senders * 8] = jnp.where(line == row, 1.0, 0.0)
        drop[...] = grid[:, : senders * 8].astype(BF16)

    rounds = [face_copies(i, i % 2 == 0) for i in range(4)]

    def start_faces(i):
        for copy in rounds[i]:
            copy.start()

    def wait_faces(i):
        for copy in rounds[i]:
            copy.wait()

    loads[0].wait()
    gather(0)
    faces(0, e, True)
    pl.semaphore_wait(barrier, senders + 1)
    send(0)
    start_faces(0)
    prepare()
    loads[1].wait()
    wait_faces(0)
    advance(0, h, e, True)
    faces(1, h, False)
    start_faces(1)
    loads[2].wait()
    loads[3].wait()
    wait_faces(1)
    advance(1, e, h, False)
    gather(1)
    send(1)
    for step in range(2):
        arrived(step).wait()
        coefficients(step, step == 1)
        medium(tiles, q, qarg, kacc, coef, gen, mom, inj, dp)
        give_back(2 + step)
        send(2 + step)
        carriers()
    saves = [
        pltpu.make_async_copy(src, dst, save_sem.at[i])
        for i, (src, dst) in enumerate(((q, q_out), (pop, n_out), (h, h_out), (e, e_out)))
    ]
    saves[0].start()
    saves[1].start()
    arrived(2).wait()
    subtract_change(2)
    faces(2, e, True)
    start_faces(2)
    wait_faces(2)
    advance(2, h, e, True)
    saves[2].start()
    faces(3, h, False)
    start_faces(3)
    wait_faces(3)
    advance(3, e, h, False)
    arrived(3).wait()
    subtract_change(3)
    saves[3].start()
    for copy in saves:
        copy.wait()


def on_device(sizes, e, h, q, n, placement, lines, gens, moment, drain):
    nfx, nfy, nma = sizes
    senders = nfy * nma
    tiles = placement.shape[1]
    any_space = pl.BlockSpec(memory_space=pl.ANY)
    smem = pl.BlockSpec(memory_space=pltpu.SMEM)
    vmem = pl.BlockSpec(memory_space=pltpu.VMEM)
    outs = pl.pallas_call(
        functools.partial(kernel, nfx, nfy, nma, tiles),
        out_shape=(
            jax.ShapeDtypeStruct((3 * PLANE, LANES), F32),
            jax.ShapeDtypeStruct((3 * PLANE, LANES), F32),
            jax.ShapeDtypeStruct((tiles * LIOU, LANES), F32),
            jax.ShapeDtypeStruct((tiles, LANES), F32),
        ),
        in_specs=[smem, smem, any_space, any_space, any_space, any_space, vmem, vmem, vmem],
        out_specs=(any_space,) * 4,
        scratch_shapes=[
            pltpu.VMEM((3 * PLANE, LANES), F32),
            pltpu.VMEM((3 * PLANE, LANES), F32),
            pltpu.VMEM((tiles * LIOU, LANES), F32),
            pltpu.VMEM((tiles * LIOU, LANES), F32),
            pltpu.VMEM((tiles * LIOU, LANES), F32),
            pltpu.VMEM((tiles, LANES), F32),
            pltpu.VMEM((tiles * 8, LANES), F32),
            pltpu.VMEM((tiles * 8, LANES), F32),
            pltpu.VMEM((tiles * 8, LANES), F32),
            pltpu.VMEM((5 * LIOU + 16, 3 * LIOU), BF16),
            pltpu.VMEM((16, 3 * LIOU), BF16),
            pltpu.VMEM((5 * LIOU + 16, LIOU), F32),
            pltpu.VMEM((senders * 8, tiles * 8), BF16),
            pltpu.VMEM((PLANE, senders * 8), BF16),
            pltpu.VMEM((PLANE, 2 * LANES), F32),
            *[pltpu.VMEM((senders * 8, LANES), F32)] * 8,
            pltpu.VMEM((4, 2 * CX, LANES), F32),
            pltpu.VMEM((4, 2 * CX, LANES), F32),
            pltpu.VMEM((4, 2 * CZ, LANES), F32),
            pltpu.VMEM((4, 2 * CZ, LANES), F32),
            pltpu.VMEM((4, 8, LANES), F32),
            pltpu.VMEM((4, 8, LANES), F32),
            pltpu.SemaphoreType.DMA((4,)),
            pltpu.SemaphoreType.DMA((4,)),
            pltpu.SemaphoreType.DMA((4,)),
            pltpu.SemaphoreType.DMA((4,)),
            pltpu.SemaphoreType.DMA((4, 3)),
            pltpu.SemaphoreType.DMA((4, 3)),
        ],
        compiler_params=pltpu.CompilerParams(collective_id=0, has_side_effects=True),
        name="maxwell_lindblad",
    )(
        lines,
        placement,
        e.reshape(3 * PLANE, LANES),
        h.reshape(3 * PLANE, LANES),
        q.reshape(tiles * LIOU, LANES),
        n.reshape(tiles, LANES),
        gens,
        moment,
        drain.reshape(1, LIOU),
    )
    return (
        outs[0].reshape(e.shape),
        outs[1].reshape(h.shape),
        outs[2].reshape(q.shape),
        outs[3].reshape(n.shape),
    )


def solution(mesh):
    sizes = tuple(mesh.shape[name] for name in ("fx", "fy", "ma"))
    field = P(None, "ma", "fx", "fy")
    owned = ("fy", "ma")
    return jax.shard_map(
        functools.partial(on_device, sizes),
        mesh=mesh,
        in_specs=(
            field,
            field,
            P("fx", owned, None, None),
            P("fx", owned, None),
            P("fx", owned),
            P("fx", owned, None, None),
            P(),
            P(),
            P(),
        ),
        out_specs=(field, field, P("fx", owned, None, None), P("fx", owned, None)),
        check_vma=False,
    )
```

```python
import functools

import jax
import jax.numpy as jnp
from jax import lax
from jax.experimental import pallas as pl
from jax.experimental.pallas import tpu as pltpu
from jax.sharding import PartitionSpec as P

MESH = pl.DeviceIdType.MESH
F32 = jnp.float32
BF16 = jnp.bfloat16
H_STEP = 0.5
DIFFUSION = 0.25
ATTENUATION = 0.1
RELAXATION = 0.5
LANES = 128
CZ, CX, LIOU = 8, 32, 64
PLANE = CZ * CX
FIRST_CUT, LAST_CUT = 1, 1
GROUP = 6


def split(x):
    hi = x.astype(BF16)
    return hi, (x - hi.astype(F32)).astype(BF16)


def stacked(x):
    hi, lo = split(x)
    return jnp.concatenate([hi, lo, hi], axis=0)


def lane_iota(shape):
    return lax.broadcasted_iota(jnp.int32, shape, len(shape) - 1)


def widen(x):
    hi, lo = split(x)
    row = lax.broadcasted_iota(jnp.int32, (LIOU, 3 * LIOU), 0)
    col = lane_iota((LIOU, 3 * LIOU))
    high = jnp.where((col < 2 * LIOU) & (col % LIOU == row), 1.0, 0.0).astype(BF16)
    low = jnp.where(col == row + 2 * LIOU, 1.0, 0.0).astype(BF16)
    out = jnp.dot(hi, high, preferred_element_type=F32) + jnp.dot(
        lo, low, preferred_element_type=F32
    )
    return out.astype(BF16)


def group_of(tiles):
    return GROUP if (tiles // 2) % GROUP == 0 else 1


def medium(first_group, last_group, tiles, q, qarg, kacc, coef, gen, mom, inj, dp):
    group = group_of(tiles)

    def run(first):
        def both(ref, p, rows, offset=0, size=None):
            size = rows if size is None else size
            base = (first + p) * 2 * rows + offset
            return jnp.concatenate(
                [ref[pl.ds(base, size), :], ref[pl.ds(base + rows, size), :]], axis=1
            )

        def put(ref, p, rows, value):
            base = (first + p) * 2 * rows
            ref[pl.ds(base, rows), :] = value[:, :LANES]
            ref[pl.ds(base + rows, rows), :] = value[:, LANES:]

        for stage in range(4):
            for p in range(group):
                arg = both(q if stage == 0 else qarg, p, LIOU)
                rows = 5 * LIOU + (16 if stage == 0 else 0)
                prod = jnp.dot(gen[:rows, :], stacked(arg), preferred_element_type=F32)
                c = [both(coef, p, 8, a, 1) for a in range(4)]
                parts = []
                for j in range(LIOU // 8):
                    b = j * 40
                    part = prod[b : b + 8]
                    for a in range(4):
                        part = part + c[a] * prod[b + 8 * a + 8 : b + 8 * a + 16]
                    parts.append(part)
                k = jnp.concatenate(parts, axis=0)
                if stage == 0:
                    put(inj, p, 8, prod[5 * LIOU : 5 * LIOU + 8])
                    put(kacc, p, LIOU, k)
                    put(qarg, p, LIOU, arg + (0.5 * H_STEP) * k)
                elif stage < 3:
                    put(kacc, p, LIOU, both(kacc, p, LIOU) + 2.0 * k)
                    step = 0.5 * H_STEP if stage == 1 else H_STEP
                    put(qarg, p, LIOU, both(q, p, LIOU) + step * k)
                else:
                    old = both(q, p, LIOU)
                    new = old + (H_STEP / 6.0) * (both(kacc, p, LIOU) + k)
                    put(q, p, LIOU, new)
                    change = jnp.dot(mom[...], stacked(new - old), preferred_element_type=F32)
                    put(dp, p, 8, change[:8])

    if last_group == first_group + 1:
        run(first_group * group)
    else:
        lax.fori_loop(first_group, last_group, lambda g, carry: (run(g * group), carry)[1], 0)


def kernel(
    nfx, nfy, nma, tiles,
    rows_in, slots_in, e_in, h_in, q_in, n_in, gens_in, moment_in, drain_in,
    e, h, q, pop, rows_s, slots_s, l_in, m_in, d_in, qarg, kacc, coef, inj, dp, gen, mom, lperm, pick, drop, grid,
    xs0, xs1, xs2, xs3, xr0, xr1, xr2, xr3, zs, zr, ls, lr, ys, yr,
    load_sem, xs_sem, xr_sem, fs_sem, fr_sem,
):
    senders = nfy * nma
    fx, fy, ma = lax.axis_index("fx"), lax.axis_index("fy"), lax.axis_index("ma")
    me = fy * nma + ma
    xs, xr = (xs0, xs1, xs2, xs3), (xr0, xr1, xr2, xr3)

    loads = [
        pltpu.make_async_copy(src, dst, load_sem.at[i])
        for i, (src, dst) in enumerate(
            (
                (e_in, e), (rows_in, rows_s), (slots_in, slots_s), (gens_in, l_in), (moment_in, m_in),
                (drain_in, d_in), (h_in, h), (n_in, pop), (q_in, q),
            )
        )
    ]
    for copy in loads:
        copy.start()

    barrier = pltpu.get_barrier_semaphore()

    def greet(d, carry):
        m = lax.rem(me + d, senders)
        pl.semaphore_signal(
            barrier, inc=1, device_id=(fx, m // nma, lax.rem(m, nma)), device_id_type=MESH
        )
        return carry

    lax.fori_loop(1, senders, greet, 0)

    has_lower, has_upper = fx > 0, fx < nfx - 1

    def greet_fx(there, d):
        @pl.when(there)
        def _():
            pl.semaphore_signal(barrier, inc=1, device_id=(fx + d, fy, ma), device_id_type=MESH)

    greet_fx(has_lower, -1)
    greet_fx(has_upper, 1)

    def meet():
        along_fx = jnp.minimum(fx, 1) + jnp.minimum(nfx - 1 - fx, 1)
        pl.semaphore_wait(barrier, senders - 1 + along_fx)

    def gather(i):
        xs[i][...] = jnp.zeros((senders * 8, LANES), F32)

        def body(m, carry):
            for k in range(2):
                r = rows_s[k, m]
                for c in range(3):
                    xs[i][pl.ds(m * 8 + k * 4 + c, 1), :] = e[pl.ds(c * PLANE + r, 1), :]
            return carry

        lax.fori_loop(0, senders, body, 0)

    def send(i):
        own = pl.ds(pl.multiple_of(me * 8, 8), 8)
        xr[i][own, :] = xs[i][own, :]

        def body(d, carry):
            m = lax.rem(me + d, senders)
            pltpu.make_async_remote_copy(
                src_ref=xs[i].at[pl.ds(pl.multiple_of(m * 8, 8), 8)],
                dst_ref=xr[i].at[own],
                send_sem=xs_sem.at[i],
                recv_sem=xr_sem.at[i],
                device_id=(fx, m // nma, lax.rem(m, nma)),
                device_id_type=MESH,
            ).start()
            return carry

        lax.fori_loop(1, senders, body, 0)

    def arrived(i):
        whole = pl.ds(0, (senders - 1) * 8)
        return pltpu.make_async_remote_copy(
            src_ref=xs[i].at[whole],
            dst_ref=xr[i].at[whole],
            send_sem=xs_sem.at[i],
            recv_sem=xr_sem.at[i],
            device_id=(fx, fy, ma),
            device_id_type=MESH,
        )

    lane8 = lane_iota((8, LANES))

    def faces(i, f, low):
        z = 0 if low else CZ - 1
        x = 0 if low else CX - 1
        y = 0 if low else LANES - 1
        for n, c in enumerate((0, 1)):
            zs[i, n * CX : (n + 1) * CX, :] = f[c * PLANE + z * CX : c * PLANE + (z + 1) * CX, :]
        for n, c in enumerate((1, 2)):
            for p in range(CZ):
                ls[i, n * CZ + p : n * CZ + p + 1, :] = f[pl.ds(c * PLANE + p * CX + x, 1), :]
        pack = jnp.zeros((8, LANES), F32)
        for n, c in enumerate((0, 2)):
            for g in range(CZ * CX // 8):
                piece = f[c * PLANE + g * 8 : c * PLANE + g * 8 + 8, :]
                pack = jnp.where(lane8 == n * 32 + g, piece[:, y : y + 1], pack)
        ys[i] = pack

    def face_copies(i, low):
        def to(index, size):
            return lax.rem(index + (size - 1 if low else 1), size)

        targets = (
            (zs, zr, (fx, fy, to(ma, nma))),
            (ls, lr, (fx - 1 if low else fx + 1, fy, ma)),
            (ys, yr, (fx, to(fy, nfy), ma)),
        )
        return [
            pltpu.make_async_remote_copy(
                src_ref=src.at[i],
                dst_ref=dst.at[i],
                send_sem=fs_sem.at[i, n],
                recv_sem=fr_sem.at[i, n],
                device_id=device,
                device_id_type=MESH,
            )
            for n, (src, dst, device) in enumerate(targets)
        ]

    row32 = lax.broadcasted_iota(jnp.int32, (CX, LANES), 0)
    lane32 = lane_iota((CX, LANES))

    def curl(i, f, forward):
        if forward:
            live = (ma < nma - 1, fx < nfx - 1, fy < nfy - 1)
        else:
            live = (ma > 0, fx > 0, fy > 0)
        live = [jnp.where(flag, 1.0, 0.0).astype(F32) for flag in live]
        shift_x, shift_y = (CX - 1, LANES - 1) if forward else (1, 1)
        edge_x, edge_y = (CX - 1, LANES - 1) if forward else (0, 0)
        packed = yr[i] * live[2]

        def plane(c, z):
            return f[c * PLANE + z * CX : c * PLANE + (z + 1) * CX, :]

        def diff(other, here):
            return other - here if forward else here - other

        for z in range(CZ):
            fields = [plane(c, z) for c in range(3)]

            def dz(c):
                n = z + (1 if forward else -1)
                if 0 <= n < CZ:
                    other = plane(c, n)
                else:
                    other = zr[i, c * CX : (c + 1) * CX, :] * live[0]
                return diff(other, fields[c])

            def dx(c):
                n = (c - 1) * CZ + z
                other = pltpu.roll(fields[c], shift_x, 0)
                other = jnp.where(row32 == edge_x, lr[i, n : n + 1, :], other)
                return diff(other, fields[c])

            def dy(c):
                n = (c // 2) * 32 + z * 4
                other = pltpu.roll(fields[c], shift_y, 1)
                column = jnp.concatenate([packed[:, n + g : n + g + 1] for g in range(4)], axis=0)
                other = jnp.where(lane32 == edge_y, column, other)
                return diff(other, fields[c])

            yield 0, z, dy(2) - dz(1)
            yield 1, z, dz(0) - dx(2)
            yield 2, z, dx(1) - dy(0)

    def advance(i, target, source, forward):
        sign = -H_STEP if forward else H_STEP
        for c, z, value in curl(i, source, forward):
            at = slice(c * PLANE + z * CX, c * PLANE + (z + 1) * CX)
            target[at, :] = target[at, :] + sign * value

    def coefficients(i, with_change):
        def body(t, carry):
            s4 = slots_s[0, t] * 4
            coef[pl.ds(t * 8, 1), :] = pop[pl.ds(t, 1), :]
            for c in range(3):
                value = xr[i][pl.ds(s4 + c, 1), :]
                if with_change:
                    value = value - dp[pl.ds(t * 8 + c, 1), :]
                coef[pl.ds(t * 8 + 1 + c, 1), :] = value
            return carry

        lax.fori_loop(0, tiles, body, 0)

    def carriers():
        now = pop[...]
        drain = jnp.concatenate([inj[t * 8 : t * 8 + 1, :] for t in range(tiles)], axis=0)
        lane = lane_iota((tiles, LANES))
        after = jnp.where(lane == LANES - 1, now, pltpu.roll(now, LANES - 1, 1))
        before = jnp.where(lane == 0, now, pltpu.roll(now, 1, 1))
        pop[...] = now + H_STEP * (
            DIFFUSION * (after - 2.0 * now + before)
            - ATTENUATION * now
            - RELAXATION * now * drain
        )

    def give_back(i):
        hi, lo = split(dp[...])
        xs[i][...] = jnp.dot(pick[...], hi, preferred_element_type=F32) + jnp.dot(
            pick[...], lo, preferred_element_type=F32
        )

    def subtract_change(i):
        back = xr[i][...]
        part = lax.broadcasted_iota(jnp.int32, back.shape, 0) % 4
        for c in range(3):
            hi, lo = split(jnp.where(part == c, back, 0.0))
            change = jnp.dot(drop[...], hi, preferred_element_type=F32) + jnp.dot(
                drop[...], lo, preferred_element_type=F32
            )
            at = slice(c * PLANE, (c + 1) * PLANE)
            e[at, :] = e[at, :] - change

    def prepare():
        for a in range(5):
            for j in range(LIOU // 8):
                lperm[j * 40 + a * 8 : j * 40 + a * 8 + 8, :] = l_in[a, j * 8 : j * 8 + 8, :]
        lperm[5 * LIOU :, :] = jnp.zeros((16, LIOU), F32)
        lperm[5 * LIOU : 5 * LIOU + 1, :] = d_in[...]
        gen[...] = widen(lperm[...])
        lperm[:16, :] = jnp.zeros((16, LIOU), F32)
        lperm[:3, :] = m_in[...]
        mom[...] = widen(lperm[:16, :])
        lane = lane_iota((8, tiles * 8))
        where_to = jnp.zeros((8, tiles * 8), jnp.int32)
        for t in range(tiles):
            where_to = jnp.where(lane // 8 == t, slots_s[0, t] * 4, where_to)
        where_to = where_to + lane % 8
        for g in range(senders):
            row = lax.broadcasted_iota(jnp.int32, (8, tiles * 8), 0) + g * 8
            lperm_free = jnp.where(where_to == row, 1.0, 0.0)
            grid[g * 8 : g * 8 + 8, : tiles * 8] = lperm_free
        pick[...] = grid[: senders * 8, : tiles * 8].astype(BF16)
        lane = lane_iota((8, senders * 8))
        line = jnp.zeros((8, senders * 8), jnp.int32)
        for m in range(senders):
            for k in range(2):
                line = jnp.where(lane // 4 == m * 2 + k, rows_s[k, m], line)
        for g in range(PLANE // 8):
            row = lax.broadcasted_iota(jnp.int32, (8, senders * 8), 0) + g * 8
            grid[g * 8 : g * 8 + 8, : senders * 8] = jnp.where(line == row, 1.0, 0.0)
        drop[...] = grid[:, : senders * 8].astype(BF16)

    rounds = [face_copies(i, i % 2 == 0) for i in range(4)]

    def sides(i):
        return (has_lower, has_upper) if i % 2 == 0 else (has_upper, has_lower)

    def start_faces(i):
        z_face, x_face, y_face = rounds[i]
        z_face.start()
        pl.when(sides(i)[0])(x_face.start)
        y_face.start()

    def wait_faces(i):
        z_face, x_face, y_face = rounds[i]
        sends, gets = sides(i)
        z_face.wait()
        y_face.wait()
        pl.when(sends)(x_face.wait_send)
        pl.when(gets)(x_face.wait_recv)

        @pl.when(jnp.logical_not(gets))
        def _():
            lr[i] = jnp.zeros((2 * CZ, LANES), F32)

    def work(first_group, last_group):
        medium(
            first_group, last_group, tiles, q, qarg, kacc, coef, gen, mom, inj, dp
        )

    groups = tiles // 2 // group_of(tiles)
    loads[0].wait()
    loads[1].wait()
    gather(0)
    faces(0, e, True)
    meet()
    send(0)
    start_faces(0)
    for copy in loads[2:6]:
        copy.wait()
    prepare()
    loads[6].wait()
    wait_faces(0)
    advance(0, h, e, True)
    faces(1, h, False)
    start_faces(1)
    loads[7].wait()
    loads[8].wait()
    arrived(0).wait()
    coefficients(0, False)
    work(0, FIRST_CUT)
    wait_faces(1)
    advance(1, e, h, False)
    gather(1)
    send(1)
    work(FIRST_CUT, groups)
    give_back(2)
    send(2)
    carriers()
    arrived(1).wait()
    coefficients(1, True)
    work(0, groups - LAST_CUT)
    arrived(2).wait()
    subtract_change(2)
    faces(2, e, True)
    start_faces(2)
    work(groups - LAST_CUT, groups)
    give_back(3)
    send(3)
    carriers()
    wait_faces(2)
    advance(2, h, e, True)
    faces(3, h, False)
    start_faces(3)
    wait_faces(3)
    advance(3, e, h, False)
    arrived(3).wait()
    subtract_change(3)


def save(e, h, q, pop, e_out, h_out, q_out, n_out, sem):
    copies = [
        pltpu.make_async_copy(src, dst, sem.at[i])
        for i, (src, dst) in enumerate(((q, q_out), (e, e_out), (h, h_out), (pop, n_out)))
    ]
    for copy in copies:
        copy.start()
    for copy in copies:
        copy.wait()


def on_device(sizes, e, h, q, n, placement, lines, gens, moment, drain):
    nfx, nfy, nma = sizes
    senders = nfy * nma
    tiles = placement.shape[1]
    hbm = pl.BlockSpec(memory_space=pltpu.HBM)
    vmem = pl.BlockSpec(memory_space=pltpu.VMEM)
    shapes = ((3 * PLANE, LANES), (3 * PLANE, LANES), (tiles * LIOU, LANES), (tiles, LANES))
    outs = pl.pallas_call(
        functools.partial(kernel, nfx, nfy, nma, tiles),
        out_shape=tuple(jax.ShapeDtypeStruct(shape, F32) for shape in shapes),
        in_specs=[hbm] * 9,
        out_specs=(vmem,) * 4,
        scratch_shapes=[
            pltpu.SMEM((2, senders), jnp.int32),
            pltpu.SMEM((1, tiles), jnp.int32),
            pltpu.VMEM((5, LIOU, LIOU), F32),
            pltpu.VMEM((3, LIOU), F32),
            pltpu.VMEM((1, LIOU), F32),
            pltpu.VMEM((tiles * LIOU, LANES), F32),
            pltpu.VMEM((tiles * LIOU, LANES), F32),
            pltpu.VMEM((tiles * 8, LANES), F32),
            pltpu.VMEM((tiles * 8, LANES), F32),
            pltpu.VMEM((tiles * 8, LANES), F32),
            pltpu.VMEM((5 * LIOU + 16, 3 * LIOU), BF16),
            pltpu.VMEM((16, 3 * LIOU), BF16),
            pltpu.VMEM((5 * LIOU + 16, LIOU), F32),
            pltpu.VMEM((senders * 8, tiles * 8), BF16),
            pltpu.VMEM((PLANE, senders * 8), BF16),
            pltpu.VMEM((PLANE, 2 * LANES), F32),
            *[pltpu.VMEM((senders * 8, LANES), F32)] * 8,
            pltpu.VMEM((4, 2 * CX, LANES), F32),
            pltpu.VMEM((4, 2 * CX, LANES), F32),
            pltpu.VMEM((4, 2 * CZ, LANES), F32),
            pltpu.VMEM((4, 2 * CZ, LANES), F32),
            pltpu.VMEM((4, 8, LANES), F32),
            pltpu.VMEM((4, 8, LANES), F32),
            pltpu.SemaphoreType.DMA((9,)),
            pltpu.SemaphoreType.DMA((4,)),
            pltpu.SemaphoreType.DMA((4,)),
            pltpu.SemaphoreType.DMA((4, 3)),
            pltpu.SemaphoreType.DMA((4, 3)),
        ],
        compiler_params=pltpu.CompilerParams(collective_id=0, has_side_effects=True, vmem_limit_bytes=24 << 20),
        name="maxwell_lindblad",
    )(*[pltpu.with_memory_space_constraint(x, pltpu.HBM) for x in (
        jnp.swapaxes(lines[0, 0], 0, 1),
        placement,
        e.reshape(3 * PLANE, LANES),
        h.reshape(3 * PLANE, LANES),
        q.reshape(tiles * LIOU, LANES),
        n.reshape(tiles, LANES),
        gens,
        moment,
        drain.reshape(1, LIOU),
    )])
    outs = pl.pallas_call(
        save,
        out_shape=tuple(jax.ShapeDtypeStruct(shape, F32) for shape in shapes),
        in_specs=[vmem] * 4,
        out_specs=(hbm,) * 4,
        scratch_shapes=[pltpu.SemaphoreType.DMA((4,))],
        compiler_params=pltpu.CompilerParams(vmem_limit_bytes=1 << 20),
        name="save",
    )(*outs)
    return (
        outs[0].reshape(e.shape),
        outs[1].reshape(h.shape),
        outs[2].reshape(q.shape),
        outs[3].reshape(n.shape),
    )


def solution(mesh):
    sizes = tuple(mesh.shape[name] for name in ("fx", "fy", "ma"))
    field = P(None, "ma", "fx", "fy")
    owned = ("fy", "ma")
    return jax.shard_map(
        functools.partial(on_device, sizes),
        mesh=mesh,
        in_specs=(
            field,
            field,
            P("fx", owned, None, None),
            P("fx", owned, None),
            P("fx", owned),
            P("fx", owned, None, None),
            P(),
            P(),
            P(),
        ),
        out_specs=(field, field, P("fx", owned, None, None), P("fx", owned, None)),
        check_vma=False,
    )
```

```python
import functools

import jax
import jax.numpy as jnp
from jax import lax
from jax.experimental import pallas as pl
from jax.experimental.pallas import tpu as pltpu
from jax.sharding import PartitionSpec as P

MESH = pl.DeviceIdType.MESH
F32 = jnp.float32
BF16 = jnp.bfloat16
H_STEP = 0.5
DIFFUSION = 0.25
ATTENUATION = 0.1
RELAXATION = 0.5
LANES = 128
CZ, CX, LIOU = 8, 32, 64
PLANE = CZ * CX


def split(x):
    hi = x.astype(BF16)
    return hi, (x - hi.astype(F32)).astype(BF16)


def stacked(x):
    hi, lo = split(x)
    return jnp.concatenate([hi, lo, hi], axis=0)


def lane_iota(shape):
    return lax.broadcasted_iota(jnp.int32, shape, len(shape) - 1)


def widen(x):
    hi, lo = split(x)
    row = lax.broadcasted_iota(jnp.int32, (LIOU, 3 * LIOU), 0)
    col = lane_iota((LIOU, 3 * LIOU))
    high = jnp.where((col < 2 * LIOU) & (col % LIOU == row), 1.0, 0.0).astype(BF16)
    low = jnp.where(col == row + 2 * LIOU, 1.0, 0.0).astype(BF16)
    out = jnp.dot(hi, high, preferred_element_type=F32) + jnp.dot(
        lo, low, preferred_element_type=F32
    )
    return out.astype(BF16)


def both(ref, p, rows, offset=0, size=None):
    size = rows if size is None else size
    base = p * 2 * rows + offset
    return jnp.concatenate(
        [ref[base : base + size, :], ref[base + rows : base + rows + size, :]], axis=1
    )


def put(ref, p, rows, value):
    base = p * 2 * rows
    ref[base : base + rows, :] = value[:, :LANES]
    ref[base + rows : base + 2 * rows, :] = value[:, LANES:]


def first_products(tiles, q, pop, gen, inj, made):
    for p in range(tiles // 2):
        prod = jnp.dot(gen[...], stacked(both(q, p, LIOU)), preferred_element_type=F32)
        n = both(pop, p, 1)
        free = [prod[b : b + 8] + n * prod[b + 8 : b + 16] for b in range(0, 5 * LIOU, 40)]
        put(made[0], p, LIOU, jnp.concatenate(free, axis=0))
        for a in range(1, 4):
            part = [prod[b + 8 * a + 8 : b + 8 * a + 16] for b in range(0, 5 * LIOU, 40)]
            put(made[a], p, LIOU, jnp.concatenate(part, axis=0))
        put(inj, p, 8, prod[5 * LIOU : 5 * LIOU + 8])


def medium(stage, tiles, q, qarg, kacc, coef, gen, mom, made, dp):
    for p in range(tiles // 2):
        c = [both(coef, p, 8, a, 1) for a in range(4)]
        if stage == 0:
            k = both(made[0], p, LIOU)
            for a in range(1, 4):
                k = k + c[a] * both(made[a], p, LIOU)
            put(kacc, p, LIOU, k)
            put(qarg, p, LIOU, both(q, p, LIOU) + (0.5 * H_STEP) * k)
            continue
        prod = jnp.dot(
            gen[: 5 * LIOU, :], stacked(both(qarg, p, LIOU)), preferred_element_type=F32
        )
        parts = []
        for j in range(LIOU // 8):
            b = j * 40
            part = prod[b : b + 8]
            for a in range(4):
                part = part + c[a] * prod[b + 8 * a + 8 : b + 8 * a + 16]
            parts.append(part)
        k = jnp.concatenate(parts, axis=0)
        if stage < 3:
            put(kacc, p, LIOU, both(kacc, p, LIOU) + 2.0 * k)
            step = 0.5 * H_STEP if stage == 1 else H_STEP
            put(qarg, p, LIOU, both(q, p, LIOU) + step * k)
        else:
            old = both(q, p, LIOU)
            new = old + (H_STEP / 6.0) * (both(kacc, p, LIOU) + k)
            put(q, p, LIOU, new)
            change = jnp.dot(mom[...], stacked(new - old), preferred_element_type=F32)
            put(dp, p, 8, change[:8])


def kernel(
    nfx, nfy, nma, tiles,
    rows_in, slots_in, e_in, h_in, q_in, n_in, gens_in, moment_in, drain_in,
    e, h, q, pop, rows_s, slots_s, l_in, m_in, d_in, qarg, kacc, coef, inj, dp, made0, made1, made2, made3, gen, mom, lperm, pick, drop, grid,
    xs0, xs1, xs2, xs3, xr0, xr1, xr2, xr3, zs, zr, ls, lr, ys, yr,
    load_sem, xs_sem, xr_sem, fs_sem, fr_sem,
):
    senders = nfy * nma
    fx, fy, ma = lax.axis_index("fx"), lax.axis_index("fy"), lax.axis_index("ma")
    me = fy * nma + ma
    xs, xr = (xs0, xs1, xs2, xs3), (xr0, xr1, xr2, xr3)

    loads = [
        pltpu.make_async_copy(src, dst, load_sem.at[i])
        for i, (src, dst) in enumerate(
            (
                (e_in, e), (rows_in, rows_s), (slots_in, slots_s), (gens_in, l_in), (moment_in, m_in),
                (drain_in, d_in), (h_in, h), (n_in, pop), (q_in, q),
            )
        )
    ]
    for copy in loads:
        copy.start()

    barrier = pltpu.get_barrier_semaphore()

    def greet(d, carry):
        m = lax.rem(me + d, senders)
        pl.semaphore_signal(
            barrier, inc=1, device_id=(fx, m // nma, lax.rem(m, nma)), device_id_type=MESH
        )
        return carry

    lax.fori_loop(1, senders, greet, 0)

    has_lower, has_upper = fx > 0, fx < nfx - 1

    def greet_fx(there, d):
        @pl.when(there)
        def _():
            pl.semaphore_signal(barrier, inc=1, device_id=(fx + d, fy, ma), device_id_type=MESH)

    greet_fx(has_lower, -1)
    greet_fx(has_upper, 1)

    def meet():
        along_fx = jnp.minimum(fx, 1) + jnp.minimum(nfx - 1 - fx, 1)
        pl.semaphore_wait(barrier, senders - 1 + along_fx)

    def gather(i):
        xs[i][...] = jnp.zeros((senders * 8, LANES), F32)

        def body(m, carry):
            for k in range(2):
                r = rows_s[k, m]
                for c in range(3):
                    xs[i][pl.ds(m * 8 + k * 4 + c, 1), :] = e[pl.ds(c * PLANE + r, 1), :]
            return carry

        lax.fori_loop(0, senders, body, 0)

    def send(i):
        own = pl.ds(pl.multiple_of(me * 8, 8), 8)
        xr[i][own, :] = xs[i][own, :]

        def body(d, carry):
            m = lax.rem(me + d, senders)
            pltpu.make_async_remote_copy(
                src_ref=xs[i].at[pl.ds(pl.multiple_of(m * 8, 8), 8)],
                dst_ref=xr[i].at[own],
                send_sem=xs_sem.at[i],
                recv_sem=xr_sem.at[i],
                device_id=(fx, m // nma, lax.rem(m, nma)),
                device_id_type=MESH,
            ).start()
            return carry

        lax.fori_loop(1, senders, body, 0)

    def arrived(i):
        whole = pl.ds(0, (senders - 1) * 8)
        return pltpu.make_async_remote_copy(
            src_ref=xs[i].at[whole],
            dst_ref=xr[i].at[whole],
            send_sem=xs_sem.at[i],
            recv_sem=xr_sem.at[i],
            device_id=(fx, fy, ma),
            device_id_type=MESH,
        )

    lane8 = lane_iota((8, LANES))

    def faces(i, f, low):
        z = 0 if low else CZ - 1
        x = 0 if low else CX - 1
        y = 0 if low else LANES - 1
        for n, c in enumerate((0, 1)):
            zs[i, n * CX : (n + 1) * CX, :] = f[c * PLANE + z * CX : c * PLANE + (z + 1) * CX, :]
        for n, c in enumerate((1, 2)):
            for p in range(CZ):
                ls[i, n * CZ + p : n * CZ + p + 1, :] = f[pl.ds(c * PLANE + p * CX + x, 1), :]
        pack = jnp.zeros((8, LANES), F32)
        for n, c in enumerate((0, 2)):
            for g in range(CZ * CX // 8):
                piece = f[c * PLANE + g * 8 : c * PLANE + g * 8 + 8, :]
                pack = jnp.where(lane8 == n * 32 + g, piece[:, y : y + 1], pack)
        ys[i] = pack

    def face_copies(i, low):
        def to(index, size):
            return lax.rem(index + (size - 1 if low else 1), size)

        targets = (
            (zs, zr, (fx, fy, to(ma, nma))),
            (ls, lr, (fx - 1 if low else fx + 1, fy, ma)),
            (ys, yr, (fx, to(fy, nfy), ma)),
        )
        return [
            pltpu.make_async_remote_copy(
                src_ref=src.at[i],
                dst_ref=dst.at[i],
                send_sem=fs_sem.at[i, n],
                recv_sem=fr_sem.at[i, n],
                device_id=device,
                device_id_type=MESH,
            )
            for n, (src, dst, device) in enumerate(targets)
        ]

    row32 = lax.broadcasted_iota(jnp.int32, (CX, LANES), 0)
    lane32 = lane_iota((CX, LANES))

    def curl(i, f, forward):
        if forward:
            live = (ma < nma - 1, fx < nfx - 1, fy < nfy - 1)
        else:
            live = (ma > 0, fx > 0, fy > 0)
        live = [jnp.where(flag, 1.0, 0.0).astype(F32) for flag in live]
        shift_x, shift_y = (CX - 1, LANES - 1) if forward else (1, 1)
        edge_x, edge_y = (CX - 1, LANES - 1) if forward else (0, 0)
        packed = yr[i] * live[2]

        def plane(c, z):
            return f[c * PLANE + z * CX : c * PLANE + (z + 1) * CX, :]

        def diff(other, here):
            return other - here if forward else here - other

        for z in range(CZ):
            fields = [plane(c, z) for c in range(3)]

            def dz(c):
                n = z + (1 if forward else -1)
                if 0 <= n < CZ:
                    other = plane(c, n)
                else:
                    other = zr[i, c * CX : (c + 1) * CX, :] * live[0]
                return diff(other, fields[c])

            def dx(c):
                n = (c - 1) * CZ + z
                other = pltpu.roll(fields[c], shift_x, 0)
                other = jnp.where(row32 == edge_x, lr[i, n : n + 1, :], other)
                return diff(other, fields[c])

            def dy(c):
                n = (c // 2) * 32 + z * 4
                other = pltpu.roll(fields[c], shift_y, 1)
                column = jnp.concatenate([packed[:, n + g : n + g + 1] for g in range(4)], axis=0)
                other = jnp.where(lane32 == edge_y, column, other)
                return diff(other, fields[c])

            yield 0, z, dy(2) - dz(1)
            yield 1, z, dz(0) - dx(2)
            yield 2, z, dx(1) - dy(0)

    def advance(i, target, source, forward):
        sign = -H_STEP if forward else H_STEP
        for c, z, value in curl(i, source, forward):
            at = slice(c * PLANE + z * CX, c * PLANE + (z + 1) * CX)
            target[at, :] = target[at, :] + sign * value

    def coefficients(i, with_change):
        def body(t, carry):
            first = slots_s[0, t] * 4
            coef[pl.ds(t * 8, 1), :] = pop[pl.ds(t, 1), :]
            for c in range(3):
                value = xr[i][pl.ds(first + c, 1), :]
                if with_change:
                    value = value - dp[pl.ds(t * 8 + c, 1), :]
                coef[pl.ds(t * 8 + 1 + c, 1), :] = value
            return carry

        lax.fori_loop(0, tiles, body, 0)

    def carriers():
        now = pop[...]
        drain = jnp.concatenate([inj[t * 8 : t * 8 + 1, :] for t in range(tiles)], axis=0)
        lane = lane_iota((tiles, LANES))
        after = jnp.where(lane == LANES - 1, now, pltpu.roll(now, LANES - 1, 1))
        before = jnp.where(lane == 0, now, pltpu.roll(now, 1, 1))
        pop[...] = now + H_STEP * (
            DIFFUSION * (after - 2.0 * now + before)
            - ATTENUATION * now
            - RELAXATION * now * drain
        )

    def give_back(i):
        hi, lo = split(dp[...])
        xs[i][...] = jnp.dot(pick[...], hi, preferred_element_type=F32) + jnp.dot(
            pick[...], lo, preferred_element_type=F32
        )

    def subtract_change(i):
        back = xr[i][...]
        part = lax.broadcasted_iota(jnp.int32, back.shape, 0) % 4
        for c in range(3):
            hi, lo = split(jnp.where(part == c, back, 0.0))
            change = jnp.dot(drop[...], hi, preferred_element_type=F32) + jnp.dot(
                drop[...], lo, preferred_element_type=F32
            )
            at = slice(c * PLANE, (c + 1) * PLANE)
            e[at, :] = e[at, :] - change

    def prepare():
        for a in range(5):
            for j in range(LIOU // 8):
                lperm[j * 40 + a * 8 : j * 40 + a * 8 + 8, :] = l_in[a, j * 8 : j * 8 + 8, :]
        lperm[5 * LIOU :, :] = jnp.zeros((16, LIOU), F32)
        lperm[5 * LIOU : 5 * LIOU + 1, :] = d_in[...]
        gen[...] = widen(lperm[...])
        lperm[:16, :] = jnp.zeros((16, LIOU), F32)
        lperm[:3, :] = m_in[...]
        mom[...] = widen(lperm[:16, :])
        lane = lane_iota((8, tiles * 8))
        where_to = jnp.zeros((8, tiles * 8), jnp.int32)
        for t in range(tiles):
            where_to = jnp.where(lane // 8 == t, slots_s[0, t] * 4, where_to)
        where_to = where_to + lane % 8
        for g in range(senders):
            row = lax.broadcasted_iota(jnp.int32, (8, tiles * 8), 0) + g * 8
            lperm_free = jnp.where(where_to == row, 1.0, 0.0)
            grid[g * 8 : g * 8 + 8, : tiles * 8] = lperm_free
        pick[...] = grid[: senders * 8, : tiles * 8].astype(BF16)
        lane = lane_iota((8, senders * 8))
        line = jnp.zeros((8, senders * 8), jnp.int32)
        for m in range(senders):
            for k in range(2):
                line = jnp.where(lane // 4 == m * 2 + k, rows_s[k, m], line)
        for g in range(PLANE // 8):
            row = lax.broadcasted_iota(jnp.int32, (8, senders * 8), 0) + g * 8
            grid[g * 8 : g * 8 + 8, : senders * 8] = jnp.where(line == row, 1.0, 0.0)
        drop[...] = grid[:, : senders * 8].astype(BF16)

    rounds = [face_copies(i, i % 2 == 0) for i in range(4)]

    def sides(i):
        return (has_lower, has_upper) if i % 2 == 0 else (has_upper, has_lower)

    def start_faces(i):
        z_face, x_face, y_face = rounds[i]
        z_face.start()
        pl.when(sides(i)[0])(x_face.start)
        y_face.start()

    def wait_faces(i):
        z_face, x_face, y_face = rounds[i]
        sends, gets = sides(i)
        z_face.wait()
        y_face.wait()
        pl.when(sends)(x_face.wait_send)
        pl.when(gets)(x_face.wait_recv)

        @pl.when(jnp.logical_not(gets))
        def _():
            lr[i] = jnp.zeros((2 * CZ, LANES), F32)

    made = (made0, made1, made2, made3)

    def work(stages):
        for stage in stages:
            medium(stage, tiles, q, qarg, kacc, coef, gen, mom, made, dp)

    loads[0].wait()
    loads[1].wait()
    gather(0)
    meet()
    send(0)
    faces(0, e, True)
    start_faces(0)
    for copy in loads[2:6]:
        copy.wait()
    prepare()
    loads[6].wait()
    wait_faces(0)
    advance(0, h, e, True)
    faces(1, h, False)
    start_faces(1)
    loads[7].wait()
    loads[8].wait()
    first_products(tiles, q, pop, gen, inj, made)
    arrived(0).wait()
    coefficients(0, False)
    work((0,))
    wait_faces(1)
    advance(1, e, h, False)
    gather(1)
    send(1)
    work((1, 2, 3))
    give_back(2)
    send(2)
    carriers()
    first_products(tiles, q, pop, gen, inj, made)
    arrived(1).wait()
    coefficients(1, True)
    work((0, 1, 2, 3))
    arrived(2).wait()
    subtract_change(2)
    faces(2, e, True)
    start_faces(2)
    give_back(3)
    send(3)
    carriers()
    wait_faces(2)
    advance(2, h, e, True)
    faces(3, h, False)
    start_faces(3)
    wait_faces(3)
    advance(3, e, h, False)
    arrived(3).wait()
    subtract_change(3)


def save(e, h, q, pop, e_out, h_out, q_out, n_out, sem):
    copies = [
        pltpu.make_async_copy(src, dst, sem.at[i])
        for i, (src, dst) in enumerate(((q, q_out), (e, e_out), (h, h_out), (pop, n_out)))
    ]
    for copy in copies:
        copy.start()
    for copy in copies:
        copy.wait()


def on_device(sizes, e, h, q, n, placement, lines, gens, moment, drain):
    nfx, nfy, nma = sizes
    senders = nfy * nma
    tiles = placement.shape[1]
    hbm = pl.BlockSpec(memory_space=pltpu.HBM)
    vmem = pl.BlockSpec(memory_space=pltpu.VMEM)
    shapes = ((3 * PLANE, LANES), (3 * PLANE, LANES), (tiles * LIOU, LANES), (tiles, LANES))
    outs = pl.pallas_call(
        functools.partial(kernel, nfx, nfy, nma, tiles),
        out_shape=tuple(jax.ShapeDtypeStruct(shape, F32) for shape in shapes),
        in_specs=[hbm] * 9,
        out_specs=(vmem,) * 4,
        scratch_shapes=[
            pltpu.SMEM((2, senders), jnp.int32),
            pltpu.SMEM((1, tiles), jnp.int32),
            pltpu.VMEM((5, LIOU, LIOU), F32),
            pltpu.VMEM((3, LIOU), F32),
            pltpu.VMEM((1, LIOU), F32),
            pltpu.VMEM((tiles * LIOU, LANES), F32),
            pltpu.VMEM((tiles * LIOU, LANES), F32),
            pltpu.VMEM((tiles * 8, LANES), F32),
            pltpu.VMEM((tiles * 8, LANES), F32),
            pltpu.VMEM((tiles * 8, LANES), F32),
            *[pltpu.VMEM((tiles * LIOU, LANES), F32)] * 4,
            pltpu.VMEM((5 * LIOU + 16, 3 * LIOU), BF16),
            pltpu.VMEM((16, 3 * LIOU), BF16),
            pltpu.VMEM((5 * LIOU + 16, LIOU), F32),
            pltpu.VMEM((senders * 8, tiles * 8), BF16),
            pltpu.VMEM((PLANE, senders * 8), BF16),
            pltpu.VMEM((PLANE, 2 * LANES), F32),
            *[pltpu.VMEM((senders * 8, LANES), F32)] * 8,
            pltpu.VMEM((4, 2 * CX, LANES), F32),
            pltpu.VMEM((4, 2 * CX, LANES), F32),
            pltpu.VMEM((4, 2 * CZ, LANES), F32),
            pltpu.VMEM((4, 2 * CZ, LANES), F32),
            pltpu.VMEM((4, 8, LANES), F32),
            pltpu.VMEM((4, 8, LANES), F32),
            pltpu.SemaphoreType.DMA((9,)),
            pltpu.SemaphoreType.DMA((4,)),
            pltpu.SemaphoreType.DMA((4,)),
            pltpu.SemaphoreType.DMA((4, 3)),
            pltpu.SemaphoreType.DMA((4, 3)),
        ],
        compiler_params=pltpu.CompilerParams(collective_id=0, has_side_effects=True, vmem_limit_bytes=24 << 20),
        name="maxwell_lindblad",
    )(*[pltpu.with_memory_space_constraint(x, pltpu.HBM) for x in (
        jnp.swapaxes(lines[0, 0], 0, 1),
        placement,
        e.reshape(3 * PLANE, LANES),
        h.reshape(3 * PLANE, LANES),
        q.reshape(tiles * LIOU, LANES),
        n.reshape(tiles, LANES),
        gens,
        moment,
        drain.reshape(1, LIOU),
    )])
    outs = pl.pallas_call(
        save,
        out_shape=tuple(jax.ShapeDtypeStruct(shape, F32) for shape in shapes),
        in_specs=[vmem] * 4,
        out_specs=(hbm,) * 4,
        scratch_shapes=[pltpu.SemaphoreType.DMA((4,))],
        compiler_params=pltpu.CompilerParams(vmem_limit_bytes=1 << 20),
        name="save",
    )(*outs)
    return (
        outs[0].reshape(e.shape),
        outs[1].reshape(h.shape),
        outs[2].reshape(q.shape),
        outs[3].reshape(n.shape),
    )


def solution(mesh):
    sizes = tuple(mesh.shape[name] for name in ("fx", "fy", "ma"))
    field = P(None, "ma", "fx", "fy")
    owned = ("fy", "ma")
    return jax.shard_map(
        functools.partial(on_device, sizes),
        mesh=mesh,
        in_specs=(
            field,
            field,
            P("fx", owned, None, None),
            P("fx", owned, None),
            P("fx", owned),
            P("fx", owned, None, None),
            P(),
            P(),
            P(),
        ),
        out_specs=(field, field, P("fx", owned, None, None), P("fx", owned, None)),
        check_vma=False,
    )
```

```python
import functools

import jax
import jax.numpy as jnp
from jax import lax
from jax.experimental import pallas as pl
from jax.experimental.pallas import tpu as pltpu
from jax.sharding import PartitionSpec as P

MESH = pl.DeviceIdType.MESH
F32 = jnp.float32
BF16 = jnp.bfloat16
H_STEP = 0.5
DIFFUSION = 0.25
ATTENUATION = 0.1
RELAXATION = 0.5
LANES = 128
CZ, CX, LIOU = 8, 32, 64
PLANE = CZ * CX


def split(x):
    hi = x.astype(BF16)
    return hi, (x - hi.astype(F32)).astype(BF16)


def stacked(x):
    hi, lo = split(x)
    return jnp.concatenate([hi, lo, hi], axis=0)


def lane_iota(shape):
    return lax.broadcasted_iota(jnp.int32, shape, len(shape) - 1)


def widen(x):
    hi, lo = split(x)
    row = lax.broadcasted_iota(jnp.int32, (LIOU, 3 * LIOU), 0)
    col = lane_iota((LIOU, 3 * LIOU))
    high = jnp.where((col < 2 * LIOU) & (col % LIOU == row), 1.0, 0.0).astype(BF16)
    low = jnp.where(col == row + 2 * LIOU, 1.0, 0.0).astype(BF16)
    out = jnp.dot(hi, high, preferred_element_type=F32) + jnp.dot(
        lo, low, preferred_element_type=F32
    )
    return out.astype(BF16)


def both(ref, p, rows, offset=0, size=None):
    size = rows if size is None else size
    base = p * 2 * rows + offset
    return jnp.concatenate(
        [ref[base : base + size, :], ref[base + rows : base + rows + size, :]], axis=1
    )


def put(ref, p, rows, value):
    base = p * 2 * rows
    ref[base : base + rows, :] = value[:, :LANES]
    ref[base + rows : base + 2 * rows, :] = value[:, LANES:]


def first_products(tiles, q, pop, gen, inj, made):
    for p in range(tiles // 2):
        prod = jnp.dot(gen[...], stacked(both(q, p, LIOU)), preferred_element_type=F32)
        n = both(pop, p, 1)
        free = [prod[b : b + 8] + n * prod[b + 8 : b + 16] for b in range(0, 5 * LIOU, 40)]
        put(made[0], p, LIOU, jnp.concatenate(free, axis=0))
        for a in range(1, 4):
            part = [prod[b + 8 * a + 8 : b + 8 * a + 16] for b in range(0, 5 * LIOU, 40)]
            put(made[a], p, LIOU, jnp.concatenate(part, axis=0))
        put(inj, p, 8, prod[5 * LIOU : 5 * LIOU + 8])


def medium(stage, tiles, q, qarg, kacc, coef, gen, mom, made, dp):
    for p in range(tiles // 2):
        c = [both(coef, p, 8, a, 1) for a in range(4)]
        if stage == 0:
            k = both(made[0], p, LIOU)
            for a in range(1, 4):
                k = k + c[a] * both(made[a], p, LIOU)
            put(kacc, p, LIOU, k)
            put(qarg, p, LIOU, both(q, p, LIOU) + (0.5 * H_STEP) * k)
            continue
        prod = jnp.dot(
            gen[: 5 * LIOU, :], stacked(both(qarg, p, LIOU)), preferred_element_type=F32
        )
        parts = []
        for j in range(LIOU // 8):
            b = j * 40
            part = prod[b : b + 8]
            for a in range(4):
                part = part + c[a] * prod[b + 8 * a + 8 : b + 8 * a + 16]
            parts.append(part)
        k = jnp.concatenate(parts, axis=0)
        if stage < 3:
            put(kacc, p, LIOU, both(kacc, p, LIOU) + 2.0 * k)
            step = 0.5 * H_STEP if stage == 1 else H_STEP
            put(qarg, p, LIOU, both(q, p, LIOU) + step * k)
        else:
            old = both(q, p, LIOU)
            new = old + (H_STEP / 6.0) * (both(kacc, p, LIOU) + k)
            put(q, p, LIOU, new)
            change = jnp.dot(mom[...], stacked(new - old), preferred_element_type=F32)
            put(dp, p, 8, change[:8])


def kernel(
    nfx, nfy, nma, tiles,
    rows_in, slots_in, e_in, h_in, q_in, n_in, gens_in, moment_in, drain_in,
    e, h, q, pop, rows_s, slots_s, l_in, m_in, d_in, qarg, kacc, coef, inj, dp, made0, made1, made2, made3, gen, mom, lperm, pick, drop, grid,
    xs0, xs1, xs2, xs3, xr0, xr1, xr2, xr3, zs, zr, ls, lr, ys, yr,
    load_sem, xs_sem, xr_sem, fs_sem, fr_sem,
):
    senders = nfy * nma
    fx, fy, ma = lax.axis_index("fx"), lax.axis_index("fy"), lax.axis_index("ma")
    me = fy * nma + ma
    xs, xr = (xs0, xs1, xs2, xs3), (xr0, xr1, xr2, xr3)

    loads = [
        pltpu.make_async_copy(src, dst, load_sem.at[i])
        for i, (src, dst) in enumerate(
            (
                (e_in, e), (rows_in, rows_s), (slots_in, slots_s), (gens_in, l_in), (moment_in, m_in),
                (drain_in, d_in), (h_in, h), (n_in, pop), (q_in, q),
            )
        )
    ]
    for copy in loads:
        copy.start()

    barrier = pltpu.get_barrier_semaphore()

    def greet(d, carry):
        m = lax.rem(me + d, senders)
        pl.semaphore_signal(
            barrier, inc=1, device_id=(fx, m // nma, lax.rem(m, nma)), device_id_type=MESH
        )
        return carry

    lax.fori_loop(1, senders, greet, 0)

    has_lower, has_upper = fx > 0, fx < nfx - 1

    def greet_fx(there, d):
        @pl.when(there)
        def _():
            pl.semaphore_signal(barrier, inc=1, device_id=(fx + d, fy, ma), device_id_type=MESH)

    greet_fx(has_lower, -1)
    greet_fx(has_upper, 1)

    def meet():
        along_fx = jnp.minimum(fx, 1) + jnp.minimum(nfx - 1 - fx, 1)
        pl.semaphore_wait(barrier, senders - 1 + along_fx)

    def gather(i):
        xs[i][...] = jnp.zeros((senders * 8, LANES), F32)

        def body(m, carry):
            for k in range(2):
                r = rows_s[k, m]
                for c in range(3):
                    xs[i][pl.ds(m * 8 + k * 3 + c, 1), :] = e[pl.ds(c * PLANE + r, 1), :]
            return carry

        lax.fori_loop(0, senders, body, 0)

    def send(i):
        own = pl.ds(pl.multiple_of(me * 8, 8), 8)
        own6 = pl.ds(pl.multiple_of(me * 8, 8), 6)
        xr[i][own, :] = xs[i][own, :]

        def body(d, carry):
            m = lax.rem(me + d, senders)
            pltpu.make_async_remote_copy(
                src_ref=xs[i].at[pl.ds(pl.multiple_of(m * 8, 8), 6)],
                dst_ref=xr[i].at[own6],
                send_sem=xs_sem.at[i],
                recv_sem=xr_sem.at[i],
                device_id=(fx, m // nma, lax.rem(m, nma)),
                device_id_type=MESH,
            ).start()
            return carry

        lax.fori_loop(1, senders, body, 0)

    def arrived(i):
        whole = pl.ds(0, (senders - 1) * 6)
        return pltpu.make_async_remote_copy(
            src_ref=xs[i].at[whole],
            dst_ref=xr[i].at[whole],
            send_sem=xs_sem.at[i],
            recv_sem=xr_sem.at[i],
            device_id=(fx, fy, ma),
            device_id_type=MESH,
        )

    lane8 = lane_iota((8, LANES))

    def faces(i, f, low):
        z = 0 if low else CZ - 1
        x = 0 if low else CX - 1
        y = 0 if low else LANES - 1
        for n, c in enumerate((0, 1)):
            zs[i, n * CX : (n + 1) * CX, :] = f[c * PLANE + z * CX : c * PLANE + (z + 1) * CX, :]
        for n, c in enumerate((1, 2)):
            for p in range(CZ):
                ls[i, n * CZ + p : n * CZ + p + 1, :] = f[pl.ds(c * PLANE + p * CX + x, 1), :]
        pack = jnp.zeros((8, LANES), F32)
        for n, c in enumerate((0, 2)):
            for g in range(CZ * CX // 8):
                piece = f[c * PLANE + g * 8 : c * PLANE + g * 8 + 8, :]
                pack = jnp.where(lane8 == n * 32 + g, piece[:, y : y + 1], pack)
        ys[i] = pack

    def face_copies(i, low):
        def to(index, size):
            return lax.rem(index + (size - 1 if low else 1), size)

        targets = (
            (zs, zr, (fx, fy, to(ma, nma))),
            (ls, lr, (fx - 1 if low else fx + 1, fy, ma)),
            (ys, yr, (fx, to(fy, nfy), ma)),
        )
        return [
            pltpu.make_async_remote_copy(
                src_ref=src.at[i],
                dst_ref=dst.at[i],
                send_sem=fs_sem.at[i, n],
                recv_sem=fr_sem.at[i, n],
                device_id=device,
                device_id_type=MESH,
            )
            for n, (src, dst, device) in enumerate(targets)
        ]

    row32 = lax.broadcasted_iota(jnp.int32, (CX, LANES), 0)
    lane32 = lane_iota((CX, LANES))

    def curl(i, f, forward):
        if forward:
            live = (ma < nma - 1, fx < nfx - 1, fy < nfy - 1)
        else:
            live = (ma > 0, fx > 0, fy > 0)
        live = [jnp.where(flag, 1.0, 0.0).astype(F32) for flag in live]
        shift_x, shift_y = (CX - 1, LANES - 1) if forward else (1, 1)
        edge_x, edge_y = (CX - 1, LANES - 1) if forward else (0, 0)
        packed = yr[i] * live[2]

        def plane(c, z):
            return f[c * PLANE + z * CX : c * PLANE + (z + 1) * CX, :]

        def diff(other, here):
            return other - here if forward else here - other

        for z in range(CZ):
            fields = [plane(c, z) for c in range(3)]

            def dz(c):
                n = z + (1 if forward else -1)
                if 0 <= n < CZ:
                    other = plane(c, n)
                else:
                    other = zr[i, c * CX : (c + 1) * CX, :] * live[0]
                return diff(other, fields[c])

            def dx(c):
                n = (c - 1) * CZ + z
                other = pltpu.roll(fields[c], shift_x, 0)
                other = jnp.where(row32 == edge_x, lr[i, n : n + 1, :], other)
                return diff(other, fields[c])

            def dy(c):
                n = (c // 2) * 32 + z * 4
                other = pltpu.roll(fields[c], shift_y, 1)
                column = jnp.concatenate([packed[:, n + g : n + g + 1] for g in range(4)], axis=0)
                other = jnp.where(lane32 == edge_y, column, other)
                return diff(other, fields[c])

            yield 0, z, dy(2) - dz(1)
            yield 1, z, dz(0) - dx(2)
            yield 2, z, dx(1) - dy(0)

    def advance(i, target, source, forward):
        sign = -H_STEP if forward else H_STEP
        for c, z, value in curl(i, source, forward):
            at = slice(c * PLANE + z * CX, c * PLANE + (z + 1) * CX)
            target[at, :] = target[at, :] + sign * value

    def coefficients(i, with_change):
        def body(t, carry):
            first = slots_s[0, t] // 2 * 8 + slots_s[0, t] % 2 * 3
            coef[pl.ds(t * 8, 1), :] = pop[pl.ds(t, 1), :]
            for c in range(3):
                value = xr[i][pl.ds(first + c, 1), :]
                if with_change:
                    value = value - dp[pl.ds(t * 8 + c, 1), :]
                coef[pl.ds(t * 8 + 1 + c, 1), :] = value
            return carry

        lax.fori_loop(0, tiles, body, 0)

    def carriers():
        now = pop[...]
        drain = jnp.concatenate([inj[t * 8 : t * 8 + 1, :] for t in range(tiles)], axis=0)
        lane = lane_iota((tiles, LANES))
        after = jnp.where(lane == LANES - 1, now, pltpu.roll(now, LANES - 1, 1))
        before = jnp.where(lane == 0, now, pltpu.roll(now, 1, 1))
        pop[...] = now + H_STEP * (
            DIFFUSION * (after - 2.0 * now + before)
            - ATTENUATION * now
            - RELAXATION * now * drain
        )

    def give_back(i):
        hi, lo = split(dp[...])
        xs[i][...] = jnp.dot(pick[...], hi, preferred_element_type=F32) + jnp.dot(
            pick[...], lo, preferred_element_type=F32
        )

    def subtract_change(i):
        back = xr[i][...]
        part = lax.broadcasted_iota(jnp.int32, back.shape, 0) % 8
        for c in range(3):
            hi, lo = split(jnp.where((part == c) | (part == c + 3), back, 0.0))
            change = jnp.dot(drop[...], hi, preferred_element_type=F32) + jnp.dot(
                drop[...], lo, preferred_element_type=F32
            )
            at = slice(c * PLANE, (c + 1) * PLANE)
            e[at, :] = e[at, :] - change

    def prepare():
        for a in range(5):
            for j in range(LIOU // 8):
                lperm[j * 40 + a * 8 : j * 40 + a * 8 + 8, :] = l_in[a, j * 8 : j * 8 + 8, :]
        lperm[5 * LIOU :, :] = jnp.zeros((16, LIOU), F32)
        lperm[5 * LIOU : 5 * LIOU + 1, :] = d_in[...]
        gen[...] = widen(lperm[...])
        lperm[:16, :] = jnp.zeros((16, LIOU), F32)
        lperm[:3, :] = m_in[...]
        mom[...] = widen(lperm[:16, :])
        lane = lane_iota((8, tiles * 8))
        where_to = jnp.zeros((8, tiles * 8), jnp.int32)
        for t in range(tiles):
            where_to = jnp.where(lane // 8 == t, slots_s[0, t] // 2 * 8 + slots_s[0, t] % 2 * 3, where_to)
        where_to = where_to + lane % 8
        for g in range(senders):
            row = lax.broadcasted_iota(jnp.int32, (8, tiles * 8), 0) + g * 8
            lperm_free = jnp.where(where_to == row, 1.0, 0.0)
            grid[g * 8 : g * 8 + 8, : tiles * 8] = lperm_free
        pick[...] = grid[: senders * 8, : tiles * 8].astype(BF16)
        lane = lane_iota((8, senders * 8))
        line = jnp.zeros((8, senders * 8), jnp.int32)
        for m in range(senders):
            for k in range(2):
                line = jnp.where((lane // 8 == m) & (lane % 8 // 3 == k), rows_s[k, m], line)
        for g in range(PLANE // 8):
            row = lax.broadcasted_iota(jnp.int32, (8, senders * 8), 0) + g * 8
            grid[g * 8 : g * 8 + 8, : senders * 8] = jnp.where(line == row, 1.0, 0.0)
        drop[...] = grid[:, : senders * 8].astype(BF16)

    rounds = [face_copies(i, i % 2 == 0) for i in range(4)]

    def sides(i):
        return (has_lower, has_upper) if i % 2 == 0 else (has_upper, has_lower)

    def start_faces(i):
        z_face, x_face, y_face = rounds[i]
        z_face.start()
        pl.when(sides(i)[0])(x_face.start)
        y_face.start()

    def wait_faces(i):
        z_face, x_face, y_face = rounds[i]
        sends, gets = sides(i)
        z_face.wait()
        y_face.wait()
        pl.when(sends)(x_face.wait_send)
        pl.when(gets)(x_face.wait_recv)

        @pl.when(jnp.logical_not(gets))
        def _():
            lr[i] = jnp.zeros((2 * CZ, LANES), F32)

    made = (made0, made1, made2, made3)

    def work(stages):
        for stage in stages:
            medium(stage, tiles, q, qarg, kacc, coef, gen, mom, made, dp)

    loads[0].wait()
    loads[1].wait()
    gather(0)
    meet()
    send(0)
    faces(0, e, True)
    start_faces(0)
    for copy in loads[2:6]:
        copy.wait()
    prepare()
    loads[6].wait()
    wait_faces(0)
    advance(0, h, e, True)
    faces(1, h, False)
    start_faces(1)
    loads[7].wait()
    loads[8].wait()
    first_products(tiles, q, pop, gen, inj, made)
    arrived(0).wait()
    coefficients(0, False)
    work((0,))
    wait_faces(1)
    advance(1, e, h, False)
    gather(1)
    send(1)
    work((1, 2, 3))
    give_back(2)
    send(2)
    carriers()
    first_products(tiles, q, pop, gen, inj, made)
    arrived(1).wait()
    coefficients(1, True)
    work((0, 1, 2, 3))
    arrived(2).wait()
    subtract_change(2)
    faces(2, e, True)
    start_faces(2)
    give_back(3)
    send(3)
    carriers()
    wait_faces(2)
    advance(2, h, e, True)
    faces(3, h, False)
    start_faces(3)
    wait_faces(3)
    advance(3, e, h, False)
    arrived(3).wait()
    subtract_change(3)


def save(e, h, q, pop, e_out, h_out, q_out, n_out, sem):
    copies = [
        pltpu.make_async_copy(src, dst, sem.at[i])
        for i, (src, dst) in enumerate(((q, q_out), (e, e_out), (h, h_out), (pop, n_out)))
    ]
    for copy in copies:
        copy.start()
    for copy in copies:
        copy.wait()


def on_device(sizes, e, h, q, n, placement, lines, gens, moment, drain):
    nfx, nfy, nma = sizes
    senders = nfy * nma
    tiles = placement.shape[1]
    hbm = pl.BlockSpec(memory_space=pltpu.HBM)
    vmem = pl.BlockSpec(memory_space=pltpu.VMEM)
    shapes = ((3 * PLANE, LANES), (3 * PLANE, LANES), (tiles * LIOU, LANES), (tiles, LANES))
    outs = pl.pallas_call(
        functools.partial(kernel, nfx, nfy, nma, tiles),
        out_shape=tuple(jax.ShapeDtypeStruct(shape, F32) for shape in shapes),
        in_specs=[hbm] * 9,
        out_specs=(vmem,) * 4,
        scratch_shapes=[
            pltpu.SMEM((2, senders), jnp.int32),
            pltpu.SMEM((1, tiles), jnp.int32),
            pltpu.VMEM((5, LIOU, LIOU), F32),
            pltpu.VMEM((3, LIOU), F32),
            pltpu.VMEM((1, LIOU), F32),
            pltpu.VMEM((tiles * LIOU, LANES), F32),
            pltpu.VMEM((tiles * LIOU, LANES), F32),
            pltpu.VMEM((tiles * 8, LANES), F32),
            pltpu.VMEM((tiles * 8, LANES), F32),
            pltpu.VMEM((tiles * 8, LANES), F32),
            *[pltpu.VMEM((tiles * LIOU, LANES), F32)] * 4,
            pltpu.VMEM((5 * LIOU + 16, 3 * LIOU), BF16),
            pltpu.VMEM((16, 3 * LIOU), BF16),
            pltpu.VMEM((5 * LIOU + 16, LIOU), F32),
            pltpu.VMEM((senders * 8, tiles * 8), BF16),
            pltpu.VMEM((PLANE, senders * 8), BF16),
            pltpu.VMEM((PLANE, 2 * LANES), F32),
            *[pltpu.VMEM((senders * 8, LANES), F32)] * 8,
            pltpu.VMEM((4, 2 * CX, LANES), F32),
            pltpu.VMEM((4, 2 * CX, LANES), F32),
            pltpu.VMEM((4, 2 * CZ, LANES), F32),
            pltpu.VMEM((4, 2 * CZ, LANES), F32),
            pltpu.VMEM((4, 8, LANES), F32),
            pltpu.VMEM((4, 8, LANES), F32),
            pltpu.SemaphoreType.DMA((9,)),
            pltpu.SemaphoreType.DMA((4,)),
            pltpu.SemaphoreType.DMA((4,)),
            pltpu.SemaphoreType.DMA((4, 3)),
            pltpu.SemaphoreType.DMA((4, 3)),
        ],
        compiler_params=pltpu.CompilerParams(collective_id=0, has_side_effects=True, vmem_limit_bytes=24 << 20),
        name="maxwell_lindblad",
    )(*[pltpu.with_memory_space_constraint(x, pltpu.HBM) for x in (
        jnp.swapaxes(lines[0, 0], 0, 1),
        placement,
        e.reshape(3 * PLANE, LANES),
        h.reshape(3 * PLANE, LANES),
        q.reshape(tiles * LIOU, LANES),
        n.reshape(tiles, LANES),
        gens,
        moment,
        drain.reshape(1, LIOU),
    )])
    outs = pl.pallas_call(
        save,
        out_shape=tuple(jax.ShapeDtypeStruct(shape, F32) for shape in shapes),
        in_specs=[vmem] * 4,
        out_specs=(hbm,) * 4,
        scratch_shapes=[pltpu.SemaphoreType.DMA((4,))],
        compiler_params=pltpu.CompilerParams(vmem_limit_bytes=1 << 20),
        name="save",
    )(*outs)
    return (
        outs[0].reshape(e.shape),
        outs[1].reshape(h.shape),
        outs[2].reshape(q.shape),
        outs[3].reshape(n.shape),
    )


def solution(mesh):
    sizes = tuple(mesh.shape[name] for name in ("fx", "fy", "ma"))
    field = P(None, "ma", "fx", "fy")
    owned = ("fy", "ma")
    return jax.shard_map(
        functools.partial(on_device, sizes),
        mesh=mesh,
        in_specs=(
            field,
            field,
            P("fx", owned, None, None),
            P("fx", owned, None),
            P("fx", owned),
            P("fx", owned, None, None),
            P(),
            P(),
            P(),
        ),
        out_specs=(field, field, P("fx", owned, None, None), P("fx", owned, None)),
        check_vma=False,
    )
```
